32 devices in a mesh: inb: 4 (over y, x), outb: 8 (over z, core).
Axes of the slice: x: 2, y: 2, z: 4, core: 2. Of those that a mesh axis runs over, the one named last changes fastest.
Arguments:
- site_cores: float32 [2, 4, 8192, 8192], P(None, None, 'inb', 'outb')
- left_env: float32 [512, 8192], P(None, 'outb')
- outcomes: int32 [2, 512], replicated, may hold values from 0 to 3
Outputs:
- env_out: float32 [512, 8192], P('inb', 'outb')
- probabilities: float32 [2, 4, 512], P(None, None, 'inb')
- log_scale: float32 [512], P('inb')
The draws below stay inside these ranges and needn't reach their ends.
All inputs are finite; a program needn't handle non-finite values.
Results may differ from the reference program's by a relative error of at most 0.00014.
Values sent between devices are 32-bit elements; how exact they have to be, the bound alone decides.
A program may use at most 128 MiB of HBM per device.

```python
import math
import jax
import jax.numpy as jnp
from jax import lax

CHI = 8192
PHYS = 4
SITES = 2
SAMPLES = 512


def draw_site_cores(key, part):
    base_key = jax.random.fold_in(key, 11)
    entry_key = jax.random.fold_in(base_key, 1)
    scale_key = jax.random.fold_in(base_key, 2)
    entries = jax.random.normal(entry_key, (SITES, PHYS, CHI, CHI), jnp.float32)
    spread = math.log(4.0)
    group_scale = jnp.exp(jax.random.uniform(scale_key, (SITES, PHYS, 1, CHI // 64), jnp.float32, 0.0, spread))
    column_scale = jnp.repeat(group_scale, 64, axis=3)
    column_ramp = 1.0 + 2.0 * jnp.arange(CHI, dtype=jnp.float32) / CHI
    return entries * column_scale * column_ramp / math.sqrt(CHI)


def draw_left_env(key, part):
    base_key = jax.random.fold_in(key, 23)
    entries = jax.random.normal(jax.random.fold_in(base_key, 1), (SAMPLES, CHI), jnp.float32)
    return entries


def place_ends(array, key, smallest, largest):
    place = [jax.random.randint(jax.random.fold_in(key, axis), (), 0, length) for axis, length in enumerate(array.shape)]
    widest = array.shape.index(max(array.shape))
    neighbour = place[:widest] + [(place[widest] + 1) % array.shape[widest]] + place[widest + 1:]
    return array.at[tuple(place)].set(smallest).at[tuple(neighbour)].set(largest)


def setup_inputs(seed: int = 0) -> dict:
    key_list = jax.random.split(jax.random.key(seed), 4)
    site_cores = draw_site_cores(jax.random.fold_in(key_list[3], 71), 0)
    left_env = draw_left_env(jax.random.fold_in(key_list[3], 71), 0)
    outcomes = place_ends(jax.random.randint(key_list[2], (SITES, SAMPLES), 0, PHYS), jax.random.fold_in(key_list[2], 1), 0, PHYS - 1).astype(jnp.int32)
    return dict(site_cores=site_cores, left_env=left_env, outcomes=outcomes)


epsilon = 1e-06

def reference(site_cores, left_env, outcomes):
    env = left_env
    log_scale = jnp.zeros((SAMPLES,), jnp.float32)
    prob_list = []
    levels = jnp.arange(PHYS, dtype=jnp.int32)
    for site_index in range(SITES):
        candidates = jnp.einsum('sc,pcd->psd', env, site_cores[site_index], precision=lax.Precision.HIGHEST)
        mean_squares = lax.optimization_barrier(jnp.sum(candidates * candidates, axis=2)) / CHI + epsilon
        prob_list.append(mean_squares / lax.optimization_barrier(jnp.sum(mean_squares, axis=0, keepdims=True)))
        onehot = (outcomes[site_index][None, :] == levels[:, None]).astype(jnp.float32)
        chosen = lax.optimization_barrier(jnp.sum(onehot[:, :, None] * candidates, axis=0))
        chosen_mean = lax.optimization_barrier(jnp.sum(onehot * mean_squares, axis=0))
        env = chosen * lax.rsqrt(chosen_mean)[:, None]
        log_scale = log_scale + 0.5 * jnp.log(chosen_mean)
    return (env, jnp.stack(prob_list), log_scale)
```

```python
import functools

import jax
import jax.numpy as jnp
from jax import lax
from jax.experimental import pallas as pl
from jax.experimental.pallas import tpu as pltpu
from jax.experimental.layout import Layout, with_layout_constraint
from jax.sharding import PartitionSpec as P

epsilon = 1e-06
MESH = pl.DeviceIdType.MESH
PARTS = 2
SPLIT = 2


def gather_kernel(part, owners, group, x_ref, out_ref, buf, recv, send, first_send, out_sem):
    width = buf.shape[2] // group
    pieces = buf.shape[0]
    me_in, me_out = lax.axis_index("inb"), lax.axis_index("outb")
    place, member = lax.div(me_out, group), lax.rem(me_out, group)
    source = place == me_in
    ahead = jnp.logical_and(place >= me_in, place < owners - 1)
    behind = jnp.logical_and(place <= me_in, place > 0)

    def columns(index):
        return pl.ds(pl.multiple_of(index * width, width), width)

    def sibling(step):
        return lax.rem(member + step, group)

    def hop(piece, slot, out_index):
        where = buf.at[piece, :, columns(member)]
        return pltpu.make_async_remote_copy(
            src_ref=where, dst_ref=where, send_sem=send.at[piece, slot], recv_sem=recv.at[member, piece],
            device_id=(me_in, out_index), device_id_type=MESH,
        )

    def hops(piece, action):
        @pl.when(ahead)
        def _():
            action(hop(piece, 0, me_out + group))

        @pl.when(behind)
        def _():
            action(hop(piece, 1, me_out - group))

        for step in range(1, group):
            action(hop(piece, 1 + step, place * group + sibling(step)))

    def landed(index, piece):
        where = buf.at[piece, :, columns(index)]
        return pltpu.make_async_copy(where, where, recv.at[index, piece])

    def leave(index, piece):
        cols = columns(index)
        return pltpu.make_async_copy(buf.at[piece, :, cols], out_ref.at[piece, :, cols], out_sem.at[index, piece])

    barrier = pltpu.get_barrier_semaphore()

    def greet(in_index, out_index):
        pl.semaphore_signal(barrier, inc=1, device_id=(in_index, out_index), device_id_type=MESH)

    for step in range(1, group):
        greet(me_in, place * group + sibling(step))

    @pl.when(place > me_in)
    def _():
        greet(me_in, me_out - group)

    @pl.when(place < me_in)
    def _():
        greet(me_in, me_out + group)

    if part is None:
        @pl.when(source)
        def _():
            for step in range(1, owners):
                greet(lax.rem(me_in + step, owners), me_out)

    targets = group - 1 + jnp.where(ahead, 1, 0) + jnp.where(behind, 1, 0)
    if part is None:
        targets = targets + jnp.where(source, 0, 1)
    pl.semaphore_wait(barrier, targets)

    def collect(index):
        piece = me_in * SPLIT + index
        return pltpu.make_async_remote_copy(
            src_ref=x_ref.at[index], dst_ref=buf.at[piece, :, columns(member)],
            send_sem=first_send.at[index], recv_sem=recv.at[member, piece],
            device_id=(place, me_out), device_id_type=MESH,
        )

    if part is None:
        @pl.when(source)
        def _():
            for index in range(SPLIT):
                piece = me_in * SPLIT + index
                pltpu.make_async_copy(
                    x_ref.at[index], buf.at[piece, :, columns(member)], recv.at[member, piece]
                ).start()

        @pl.when(jnp.logical_not(source))
        def _():
            for index in range(SPLIT):
                collect(index).start()
    else:
        @pl.when(source)
        def _():
            for piece in range(pieces):
                pltpu.make_async_copy(
                    x_ref.at[piece // SPLIT, part, piece % SPLIT],
                    buf.at[piece, :, columns(member)], recv.at[member, piece],
                ).start()

    for piece in range(pieces):
        landed(member, piece).wait()
        hops(piece, lambda copy: copy.start())
        leave(member, piece).start()
    for piece in range(pieces):
        for step in range(1, group):
            landed(sibling(step), piece).wait()
            leave(sibling(step), piece).start()
    if part is None:
        @pl.when(jnp.logical_not(source))
        def _():
            for index in range(SPLIT):
                collect(index).wait_send()
    for piece in range(pieces):
        hops(piece, lambda copy: copy.wait_send())
        leave(member, piece).wait()
        for step in range(1, group):
            leave(sibling(step), piece).wait()


def gather_rows(x, part, owners, group, rows, width, call_id):
    pieces = owners * SPLIT
    shape = (pieces, rows // SPLIT, group * width)
    sent = pieces * (rows // SPLIT) * width * 4
    out = pl.pallas_call(
        functools.partial(gather_kernel, part, owners, group),
        out_shape=jax.ShapeDtypeStruct(shape, jnp.float32),
        in_specs=[pl.BlockSpec(memory_space=pl.ANY)],
        out_specs=pl.BlockSpec(memory_space=pl.ANY),
        scratch_shapes=[
            pltpu.VMEM(shape, jnp.float32),
            pltpu.SemaphoreType.DMA((group, pieces)),
            pltpu.SemaphoreType.DMA((pieces, 1 + group)),
            pltpu.SemaphoreType.DMA((SPLIT,)),
            pltpu.SemaphoreType.DMA((group, pieces)),
        ],
        compiler_params=pltpu.CompilerParams(collective_id=call_id, has_side_effects=True),
        cost_estimate=pl.CostEstimate(flops=0, bytes_accessed=64 * sent, transcendentals=0),
        name="gather_rows_%d" % call_id,
    )(x)
    return out.reshape(owners * rows, group * width)


def total_kernel(count, x_ref, out_ref, buf, send, recv):
    me_in, me_out = lax.axis_index("inb"), lax.axis_index("outb")
    barrier = pltpu.get_barrier_semaphore()
    for step in range(1, count):
        pl.semaphore_signal(
            barrier, inc=1, device_id=(me_in, lax.rem(me_out + step, count)), device_id_type=MESH
        )
    pl.semaphore_wait(barrier, count - 1)

    def give(step):
        return pltpu.make_async_remote_copy(
            src_ref=x_ref, dst_ref=buf.at[me_out], send_sem=send.at[step], recv_sem=recv.at[me_out],
            device_id=(me_in, lax.rem(me_out + step, count)), device_id_type=MESH,
        )

    for step in range(1, count):
        give(step).start()
    buf[me_out] = x_ref[...]
    for step in range(1, count):
        origin = lax.rem(me_out + step, count)
        pltpu.make_async_copy(x_ref, buf.at[origin], recv.at[origin]).wait()
    total = buf[0]
    for index in range(1, count):
        total = total + buf[index]
    out_ref[...] = total
    for step in range(1, count):
        give(step).wait_send()


def total_over_outb(x, count, call_id):
    height, width = x.shape
    tall, wide = -(-height // 8) * 8, -(-width // 128) * 128
    padded = jnp.pad(x, ((0, tall - height), (0, wide - width)))
    out = pl.pallas_call(
        functools.partial(total_kernel, count),
        out_shape=jax.ShapeDtypeStruct((tall, wide), jnp.float32),
        in_specs=[pl.BlockSpec(memory_space=pltpu.VMEM)],
        out_specs=pl.BlockSpec(memory_space=pltpu.VMEM),
        scratch_shapes=[
            pltpu.VMEM((count, tall, wide), jnp.float32),
            pltpu.SemaphoreType.DMA((count,)),
            pltpu.SemaphoreType.DMA((count,)),
        ],
        compiler_params=pltpu.CompilerParams(collective_id=call_id, has_side_effects=True),
        cost_estimate=pl.CostEstimate(flops=0, bytes_accessed=16_000_000, transcendentals=0),
        name="total_%d" % call_id,
    )(padded)
    return out[:height, :width]


def on_device(owners, outs, site_cores, left_env, outcomes):
    inb_index = lax.axis_index("inb")
    samples_all, width_out = left_env.shape
    sites, outcome_count = site_cores.shape[:2]
    block_rows = samples_all // owners
    rows = block_rows // PARTS
    group = outs // owners
    bond_width = width_out * outs
    levels = jnp.arange(outcome_count, dtype=jnp.int32)
    chosen_ids = lax.dynamic_slice_in_dim(outcomes, inb_index * block_rows, block_rows, 1)
    left_pieces = left_env.reshape(owners, PARTS, SPLIT, rows // SPLIT, width_out)

    log_scale = [jnp.zeros((rows,), jnp.float32)] * PARTS
    current = [left_pieces] * PARTS
    candidates = [None] * PARTS
    probs = [[None] * PARTS for _ in range(sites)]
    row_major = Layout(major_to_minor=(0, 1, 2))
    last = PARTS - 1

    def settle(site_index, part):
        squares = jnp.sum(candidates[part] * candidates[part], axis=2)
        totals = total_over_outb(squares, outs, sites * PARTS + site_index * PARTS + part)
        mean_squares = totals / bond_width + epsilon
        probs[site_index][part] = mean_squares / jnp.sum(mean_squares, axis=0, keepdims=True)
        ids = chosen_ids[site_index, part * rows : (part + 1) * rows]
        onehot = (ids[None, :] == levels[:, None]).astype(jnp.float32)
        chosen = jnp.sum(onehot[:, :, None] * candidates[part], axis=0)
        chosen_mean = jnp.sum(onehot * mean_squares, axis=0)
        log_scale[part] = log_scale[part] + 0.5 * jnp.log(chosen_mean)
        scaled = chosen * lax.rsqrt(chosen_mean)[:, None]
        current[part] = scaled.reshape(SPLIT, rows // SPLIT, width_out)

    for site_index in range(sites):
        for part in range(PARTS):
            if site_index > 0:
                settle(site_index - 1, part)
            own_cols = gather_rows(
                current[part], part if site_index == 0 else None, owners, group, rows, width_out,
                site_index * PARTS + part,
            )
            partial_terms = jnp.einsum(
                "sc,pcd->psd", own_cols, site_cores[site_index], precision=lax.Precision.HIGH
            )
            partial_terms = with_layout_constraint(partial_terms, row_major)
            if part < last:
                waiting = current if site_index == 0 else candidates
                waiting[part + 1], partial_terms = lax.optimization_barrier((waiting[part + 1], partial_terms))
            elif site_index == sites - 1:
                *candidates[:last], partial_terms = lax.optimization_barrier((*candidates[:last], partial_terms))
            summed = lax.psum_scatter(partial_terms, "inb", scatter_dimension=1, tiled=True)
            candidates[part] = with_layout_constraint(summed, row_major)
    for part in range(PARTS):
        settle(sites - 1, part)
    env_out = jnp.concatenate([x.reshape(rows, width_out) for x in current], axis=0)
    prob_stack = jnp.stack([jnp.concatenate(x, axis=1) for x in probs])
    return (env_out, prob_stack, jnp.concatenate(log_scale))


def solution(mesh):
    in_specs = (P(None, None, "inb", "outb"), P(None, "outb"), P())
    out_specs = (P("inb", "outb"), P(None, None, "inb"), P("inb"))
    return jax.shard_map(
        functools.partial(on_device, mesh.shape["inb"], mesh.shape["outb"]),
        mesh=mesh, in_specs=in_specs, out_specs=out_specs, check_vma=False,
    )
```
